32 devices in a mesh: groups: 2 (over x), azim: 16 (over z, y, core).
Axes of the slice: x: 2, y: 2, z: 4, core: 2. Of those that a mesh axis runs over, the one named last changes fastest.
Arguments:
- conserved: float32 [5, 256, 2048], P(None, ('groups', 'azim')), parts along dimension 1, may hold values from -6 to 6
- velocity: float32 [256, 2048], P(('groups', 'azim')), parts along dimension 0, may hold values from -0.8 to 0.8
- viscosity: float32 [5], replicated, may hold values from 0.02 to 0.1
- shifts: int32 [4, 64], P('groups'), parts along dimension 0, may hold values from 0 to 127
Outputs:
- advanced: float32 [5, 256, 2048], P(None, ('groups', 'azim')), parts along dimension 1
The draws below stay inside these ranges and needn't reach their ends.
There are 2 independent parts, one for each index of `groups`. The reference program is written for one: setup_inputs(seed, part) draws one part's arguments, and reference() takes and returns one part's arrays. A program takes and returns all parts, laid end to end along the dimension named above; an argument that names none is the same for every part. Nothing has to cross between parts.
All inputs are finite; a program needn't handle non-finite values.
Results may differ from the reference program's by a relative error of at most 0.0003.
Values sent between devices are 32-bit elements; how exact they have to be, the bound alone decides.
A program may use at most 64 MiB of HBM per device.

```python
import math
import jax
import jax.numpy as jnp

NR = 64
FIELDS = 5
STEPS = 2
NPHI = 128
COLS = 2048


def place_ends(array, key, low, high):
    longest = array.shape.index(max(array.shape))
    spots = []
    for shift in (0, 1):
        where = [jax.random.randint(jax.random.fold_in(key, axis), (), 0, length) for axis, length in enumerate(array.shape)]
        where[longest] = (where[longest] + shift) % array.shape[longest]
        spots.append(tuple(where))
    return array.at[spots[0]].set(low).at[spots[1]].set(high)


def levels(stream_key, dims, split, smallest, top_value):
    def one(axis_at, shards_of):
        steps = jax.random.uniform(jax.random.fold_in(jax.random.fold_in(stream_key, 6), axis_at), (shards_of,), jnp.float32, smallest / len(split), top_value / len(split))
        return jnp.repeat(jnp.exp(steps), dims[axis_at] // shards_of).reshape((-1,) + (1,) * (len(dims) - axis_at - 1))

    loudness = one(*split[0])
    for cut in split[1:]:
        loudness = loudness * one(*cut)
    return loudness


def normal_values(stream_key, dims, scale, bound, split=(), kind=jnp.bfloat16):
    drawn = scale * jax.random.normal(stream_key, dims, jnp.float32)
    if split:
        drawn = drawn * levels(stream_key, dims, split, -0.22, 0.18)
    return jnp.clip(drawn, -bound, bound).astype(kind)


def setup_inputs(seed: int = 0, part: int = 0) -> dict:
    keys = jax.random.split(jax.random.key(seed), 5)
    part_keys = jax.random.split(jax.random.fold_in(keys[4], part), 5)
    conserved = normal_values(part_keys[0], (FIELDS, NPHI, COLS), 1.0, 6.0, ((1, 16),), jnp.float32)
    velocity = jnp.clip(jax.random.uniform(part_keys[1], (NPHI, COLS), jnp.float32, -0.8, 0.8) * levels(part_keys[1], (NPHI, COLS), ((0, 16),), -0.4, 0.0), -0.8, 0.8)
    viscosity = jnp.clip(jnp.exp(jax.random.uniform(keys[2], (FIELDS,), jnp.float32, math.log(0.02), math.log(0.1))), 0.02, 0.1)
    shifts = place_ends(jax.random.randint(part_keys[3], (STEPS, NR), 0, NPHI), jax.random.fold_in(part_keys[3], 1), 0, NPHI - 1).astype(jnp.int32)
    return dict(conserved=conserved, velocity=velocity, viscosity=viscosity, shifts=shifts)


def minmod(left, right):
    return 0.5 * (jnp.sign(left) + jnp.sign(right)) * jnp.minimum(jnp.abs(left), jnp.abs(right))


def lateral_sum(inner, heights):
    width = inner.shape[2]
    height_of = jnp.arange(width, dtype=jnp.int32) % heights
    outward = jnp.concatenate([inner[:, :, heights:], inner[:, :, width - heights:]], axis=2)
    inward = jnp.concatenate([inner[:, :, :heights], inner[:, :, :width - heights]], axis=2)
    upper = jnp.concatenate([inner[:, :, 1:], inner[:, :, width - 1:]], axis=2)
    upper = jnp.where((height_of == heights - 1)[None, None, :], inner, upper)
    lower = jnp.concatenate([inner[:, :, :1], inner[:, :, :width - 1]], axis=2)
    lower = jnp.where((height_of == 0)[None, None, :], inner, lower)
    return outward + inward + upper + lower - 4.0 * inner


def tendency(ext, speed, viscosity, heights):
    count = ext.shape[1]
    diff = ext[:, 1:] - ext[:, :-1]
    slope = minmod(diff[:, :-1], diff[:, 1:])
    left_state = ext[:, 1:count - 2] + 0.5 * slope[:, 0:count - 3]
    right_state = ext[:, 2:count - 1] - 0.5 * slope[:, 1:count - 2]
    face_speed = 0.5 * (speed[1:count - 2] + speed[2:count - 1])
    flux = jnp.maximum(face_speed, 0.0) * left_state + jnp.minimum(face_speed, 0.0) * right_state
    inner = ext[:, 2:count - 2]
    azimuthal = ext[:, 3:count - 1] + ext[:, 1:count - 3] - 2.0 * inner
    lateral = lateral_sum(inner, heights)
    return -(flux[:, 1:] - flux[:, :-1]) + viscosity[:, None, None] * (azimuthal + lateral)


def wrapped(field, width):
    return jnp.concatenate([field[:, -width:], field, field[:, :width]], axis=1)


def reference(conserved, velocity, viscosity, shifts):
    state = conserved
    speed = jnp.concatenate([velocity[-2:], velocity, velocity[:2]], axis=0)
    total = state.shape[1]
    width = state.shape[2]
    heights = width // shifts.shape[1]
    for step in range(STEPS):
        first = state + tendency(wrapped(state, 2), speed, viscosity, heights)
        second = 0.75 * state + 0.25 * (first + tendency(wrapped(first, 2), speed, viscosity, heights))
        third = (1.0 / 3.0) * state + (2.0 / 3.0) * (second + tendency(wrapped(second, 2), speed, viscosity, heights))
        per_column = jnp.repeat(shifts[step], heights)
        anchor = jnp.mod(jnp.arange(total, dtype=jnp.int32)[:, None] - per_column[None, :], total).astype(jnp.int32)
        anchor = jnp.broadcast_to(anchor[None], third.shape)
        state = jnp.take_along_axis(third, anchor, axis=1)
    return state
```

```python
import functools

import jax
import jax.numpy as jnp
from jax import lax
from jax.experimental import pallas as pl
from jax.experimental.pallas import tpu as pltpu
from jax.sharding import PartitionSpec as P

STEPS = 2
OWNED = 4
LOOK = 3
LAG = 3
AHEAD = 2
LANES = 128
SUBLANES = 8


def padded(cells, sides, width):
    for axis, dim in sides:
        count = lax.axis_size(axis)
        head = lax.slice_in_dim(cells, 0, width, axis=dim)
        tail = lax.slice_in_dim(cells, cells.shape[dim] - width, cells.shape[dim], axis=dim)
        cells = jnp.concatenate(
            [
                lax.ppermute(tail, axis, [(i, (i + 1) % count) for i in range(count)]),
                cells,
                lax.ppermute(head, axis, [((i + 1) % count, i) for i in range(count)]),
            ],
            axis=dim,
        )
    return cells


def shifted(value, axis, steps):
    count = lax.axis_size(axis)
    pairs = [(source, (source + steps) % count) for source in range(count)]
    return lax.ppermute(value, axis, pairs)


def minmod(left, right):
    return 0.5 * (jnp.sign(left) + jnp.sign(right)) * jnp.minimum(jnp.abs(left), jnp.abs(right))


def lateral_sum(inner, heights):
    width = inner.shape[2]
    height_of = jnp.arange(width, dtype=jnp.int32) % heights
    outward = jnp.concatenate([inner[:, :, heights:], inner[:, :, width - heights :]], axis=2)
    inward = jnp.concatenate([inner[:, :, :heights], inner[:, :, : width - heights]], axis=2)
    upper = jnp.concatenate([inner[:, :, 1:], inner[:, :, width - 1 :]], axis=2)
    upper = jnp.where((height_of == heights - 1)[None, None, :], inner, upper)
    lower = jnp.concatenate([inner[:, :, :1], inner[:, :, : width - 1]], axis=2)
    lower = jnp.where((height_of == 0)[None, None, :], inner, lower)
    return outward + inward + upper + lower - 4.0 * inner


def tendency(ext, speed, viscosity, heights):
    count = ext.shape[1]
    diff = ext[:, 1:] - ext[:, :-1]
    slope = minmod(diff[:, :-1], diff[:, 1:])
    left_state = ext[:, 1 : count - 2] + 0.5 * slope[:, 0 : count - 3]
    right_state = ext[:, 2 : count - 1] - 0.5 * slope[:, 1 : count - 2]
    face_speed = 0.5 * (speed[1 : count - 2] + speed[2 : count - 1])
    flux = jnp.maximum(face_speed, 0.0) * left_state + jnp.minimum(face_speed, 0.0) * right_state
    inner = ext[:, 2 : count - 2]
    azimuthal = ext[:, 3 : count - 1] + ext[:, 1 : count - 3] - 2.0 * inner
    lateral = lateral_sum(inner, heights)
    return -(flux[:, 1:] - flux[:, :-1]) + viscosity[:, None, None] * (azimuthal + lateral)


def section_rim(field):
    return padded(field, (("azim", 1),), 2)


def slide_down(joined, amount, limit):
    current = joined
    level = 0
    while 1 << level < limit:
        stride = 1 << level
        taken = amount >> level & 1 == 1
        moved = jnp.concatenate(
            [jnp.zeros_like(current[:, :stride]), current[:, : current.shape[1] - stride]], axis=1
        )
        current = jnp.where(taken[None, None, :], moved, current)
        level = level + 1
    return current


def by_azimuth(conserved, velocity, viscosity, shifts):
    state = conserved
    block = state.shape[1]
    heights = state.shape[2] // shifts.shape[1]
    devices = lax.axis_size("azim")
    levels = devices.bit_length() - 1
    speed_wide = padded(velocity, (("azim", 0),), 6)
    speed_near = speed_wide[4:-4]
    for step in range(STEPS):
        first = state + tendency(section_rim(state), speed_near, viscosity, heights)
        second = 0.75 * state + 0.25 * (
            first + tendency(section_rim(first), speed_near, viscosity, heights)
        )
        third = 1.0 / 3.0 * state + 2.0 / 3.0 * (
            second + tendency(section_rim(second), speed_near, viscosity, heights)
        )
        per_column = jnp.repeat(shifts[step], heights)
        whole_blocks = per_column // block
        remainder = per_column - whole_blocks * block
        moved = third
        for level in range(levels):
            taken = whole_blocks >> level & 1 == 1
            arrived = shifted(moved, "azim", 1 << level)
            moved = jnp.where(taken[None, None, :], arrived, moved)
        preceding = shifted(moved, "azim", 1)
        joined = jnp.concatenate([preceding, moved], axis=1)
        state = slide_down(joined, remainder, block)[:, block:]
    return state


def winding(d):
    row, chip, core = d // 4, (d % 4) // 2, d % 2
    return row * 4 + ((row + chip) % 2) * 2 + core


def lateral_matrix(place, heights, n):
    total = n * OWNED
    half = OWNED // 2

    def places(axis):
        lane = lax.broadcasted_iota(jnp.int32, (3 * LANES, 2 * LANES), axis)
        height = lane % heights
        group = lane // heights
        tile, slot = group // OWNED, group % OWNED
        inner = jnp.where(slot < half, slot + OWNED, slot - OWNED)
        outer = jnp.where(slot < half, slot - OWNED, slot + OWNED)
        radius = jnp.where(tile == 0, slot, jnp.where(tile == 1, inner, outer))
        return height, radius + place * OWNED

    h_from, r_from = places(0)
    h_to, r_to = places(1)
    inside = (r_from >= 0) & (r_from < total) & (r_to >= 0) & (r_to < total)
    h_gap = jnp.abs(h_from - h_to)
    r_gap = jnp.abs(r_from - r_to)

    def one(condition):
        return jnp.where(condition, 1.0, 0.0)

    own = one(h_to == 0) + one(h_to == heights - 1) + one(r_to == 0) + one(r_to == total - 1) - 4.0
    weight = jnp.where(h_gap + r_gap == 0, own, one(h_gap + r_gap == 1))
    return jnp.where(inside, weight, 0.0).astype(jnp.bfloat16)


def disc_kernel(
    n,
    heights,
    cons,
    vel,
    visc_in,
    shifts_in,
    out,
    visc,
    shifts,
    s_own,
    u,
    ul,
    ur,
    vp,
    vn,
    t1,
    t2,
    mat,
    obuf,
    a_send,
    a_recv,
    a_own,
    h_send,
    h_recv,
    x_send,
    x_recv,
    x_own,
    o_send,
    o_recv,
    o_own,
):
    fields, block, cols = cons.shape
    azim = n * block
    me = lax.axis_index("azim")
    place = winding(me)
    inward = winding(lax.rem(place + n - 1, n))
    outward = winding(lax.rem(place + 1, n))
    middle = n // 2

    barrier = pltpu.get_barrier_semaphore()

    def greet(k, carry):
        pl.semaphore_signal(barrier, inc=1, device_id={"azim": lax.rem(me + k, n)})
        return carry

    lax.fori_loop(1, n, greet, 0)
    pl.semaphore_wait(barrier, n - 1)

    def lanes(d):
        return pl.ds(pl.multiple_of(d * LANES, LANES), LANES)

    def rows(d):
        return pl.ds(pl.multiple_of(d * block, block), block)

    def share(plane, d):
        if isinstance(plane, int) and plane == fields:
            return vel.at[:, lanes(winding(d))]
        return cons.at[plane, :, lanes(winding(d))]

    def send_to(plane, to):
        pltpu.make_async_remote_copy(
            src_ref=share(plane, to),
            dst_ref=u.at[0, plane, rows(me), :],
            send_sem=a_send.at[plane],
            recv_sem=a_recv.at[plane],
            device_id={"azim": to},
        ).start()

    def cross_to(plane, side):
        taker = winding(middle - 1 + side)
        giver = winding(middle - side)
        tile = ul if side else ur
        there = pltpu.make_async_remote_copy(
            src_ref=share(plane, giver),
            dst_ref=tile.at[0, plane, rows(me), :],
            send_sem=x_send.at[plane],
            recv_sem=x_recv.at[plane],
            device_id={"azim": taker},
        )
        here = pltpu.make_async_copy(
            share(plane, giver), tile.at[0, plane, rows(me), :], x_own.at[plane]
        )
        return taker, there, here

    def send_in(plane):
        def one(k, carry):
            send_to(plane, lax.rem(me + k, n))
            return carry

        lax.fori_loop(1, n, one, 0)
        pltpu.make_async_copy(
            share(plane, me), u.at[0, plane, rows(me), :], a_own.at[plane]
        ).start()
        for side in (0, 1):
            taker, there, here = cross_to(plane, side)
            pl.when(taker != me)(there.start)
            pl.when(taker == me)(here.start)

    send_in(fields)
    for f in range(min(LOOK, fields)):
        send_in(f)

    scalars = (
        pltpu.make_async_copy(visc_in, visc, s_own.at[0]),
        pltpu.make_async_copy(shifts_in, shifts, s_own.at[1]),
    )
    for copy in scalars:
        copy.start()

    def all_in(plane):
        others = u.at[0, plane, pl.ds(0, azim - block), :]
        return pltpu.make_async_remote_copy(
            src_ref=others,
            dst_ref=others,
            send_sem=a_send.at[plane],
            recv_sem=a_recv.at[plane],
            device_id={"azim": outward},
        )

    def cross(plane, count):
        others = ul.at[0, plane, pl.ds(0, count * block), :]
        return pltpu.make_async_remote_copy(
            src_ref=others,
            dst_ref=others,
            send_sem=x_send.at[plane],
            recv_sem=x_recv.at[plane],
            device_id={"azim": outward},
        )

    def linked(step):
        if step == 0:
            return (place > 0) & (place != middle), (place < n - 1) & (place != middle - 1)
        return place > 0, place < n - 1

    def halo(step, plane):
        inner = pltpu.make_async_remote_copy(
            src_ref=u.at[step, plane],
            dst_ref=ur.at[step, plane],
            send_sem=h_send.at[step, 0, plane],
            recv_sem=h_recv.at[step, 0, plane],
            device_id={"azim": inward},
        )
        outer = pltpu.make_async_remote_copy(
            src_ref=u.at[step, plane],
            dst_ref=ul.at[step, plane],
            send_sem=h_send.at[step, 1, plane],
            recv_sem=h_recv.at[step, 1, plane],
            device_id={"azim": outward},
        )
        return inner, outer

    def halo_start(step, plane):
        inner, outer = halo(step, plane)
        back, ahead = linked(step)
        pl.when(back)(inner.start)
        pl.when(ahead)(outer.start)

    def halo_recv(step, plane):
        inner, outer = halo(step, plane)
        back, ahead = linked(step)
        pl.when(back)(outer.wait_recv)
        pl.when(ahead)(inner.wait_recv)
        if step == 0:
            at_middle = (place == middle - 1) | (place == middle)

            @pl.when(at_middle)
            def _():
                pltpu.make_async_copy(
                    ul.at[0, plane, rows(me), :], ul.at[0, plane, rows(me), :], x_own.at[plane]
                ).wait()
                cross(plane, n - 1).wait_recv()

    def halo_sent(step, plane):
        inner, outer = halo(step, plane)
        back, ahead = linked(step)
        pl.when(back)(inner.wait_send)
        pl.when(ahead)(outer.wait_send)

    def arrive(plane):
        pltpu.make_async_copy(
            u.at[0, plane, rows(me), :], u.at[0, plane, rows(me), :], a_own.at[plane]
        ).wait()
        all_in(plane).wait_recv()
        halo_start(0, plane)
        later = LOOK if isinstance(plane, int) and plane == fields else plane + LOOK + 1
        if isinstance(later, int):
            if later < fields:
                send_in(later)
        else:
            pl.when(later < fields)(lambda: send_in(later))

    def send_out(f):
        def one(k, carry):
            to = lax.rem(me + k, n)
            pltpu.make_async_remote_copy(
                src_ref=obuf.at[f, rows(to), :],
                dst_ref=out.at[f, :, lanes(place)],
                send_sem=o_send.at[f],
                recv_sem=o_recv.at[f],
                device_id={"azim": to},
            ).start()
            return carry

        lax.fori_loop(1, n, one, 0)
        pltpu.make_async_copy(obuf.at[f, rows(me), :], out.at[f, :, lanes(place)], o_own.at[f]).start()

    def each(body, count=fields):
        def one(f, carry):
            body(f)
            return carry

        lax.fori_loop(0, count, one, 0)

    def clear(tile):
        def one(plane, carry):
            for step in range(STEPS):
                tile[step, plane] = jnp.zeros((azim, LANES), jnp.float32)
            return carry

        lax.fori_loop(0, fields + 1, one, 0)

    pl.when(place == 0)(lambda: clear(ul))
    pl.when(place == n - 1)(lambda: clear(ur))
    mat[...] = lateral_matrix(place, heights, n)

    lane = lax.broadcasted_iota(jnp.int32, (azim, LANES), 1)
    lower = lane < LANES // 2

    def tiles(step, plane):
        own, left, right = u[step, plane], ul[step, plane], ur[step, plane]
        near = jnp.concatenate([own, jnp.where(lower, right, left)], axis=1)
        return near, jnp.where(lower, left, right)

    def ahead_one(x):
        return pltpu.roll(x, azim - 1, 0)

    def back_one(x):
        return pltpu.roll(x, 1, 0)

    def halves(x):
        high = x.astype(jnp.bfloat16)
        return high, (x - high.astype(jnp.float32)).astype(jnp.bfloat16)

    def lateral(x, count):
        both = jnp.concatenate(halves(x), axis=0)
        y = jnp.dot(both, mat[: 2 * LANES, :count], preferred_element_type=jnp.float32)
        return y[:azim] + y[azim:]

    def change(x, spread, nu):
        count = spread.shape[1]
        x = x[:, :count]
        d = x - back_one(x)
        dp = ahead_one(d)
        low = jnp.minimum(d, dp)
        high = jnp.maximum(d, dp)
        half = 0.5 * (jnp.maximum(low, 0.0) + jnp.minimum(high, 0.0))
        p = vp[:, :count] * (x + half)
        q = vn[:, :count] * (x - half)
        flow = (p - q) + (ahead_one(q) - back_one(p))
        return x + (nu * ((dp - d) + spread) - flow)

    def advance(step, f):
        nu = visc[f]
        near, far = tiles(step, f)
        rim = mat[2 * LANES :, :]
        spread = lateral(near, 2 * LANES) + jnp.dot(
            jnp.concatenate(halves(far), axis=1),
            jnp.concatenate([rim, rim], axis=0),
            preferred_element_type=jnp.float32,
        )
        t1[...] = change(near, spread, nu)
        x = t1[...]
        t2[...] = 0.75 * near + 0.25 * change(x, lateral(x, 2 * LANES), nu)
        x = t2[...]
        y = (1.0 / 3.0) * near[:, :LANES] + (2.0 / 3.0) * change(x, lateral(x, LANES), nu)
        slot = lax.broadcasted_iota(jnp.int32, (SUBLANES, LANES), 1) // heights
        amount = jnp.zeros((SUBLANES, LANES), jnp.int32)
        for r in range(OWNED):
            amount = jnp.where(slot == r, shifts[step, place * OWNED + r], amount)
        for bit in range(azim.bit_length() - 1):
            taken = ((amount >> bit) & 1 == 1)[:1]
            taken = jnp.broadcast_to(taken, (azim, LANES))
            y = jnp.where(taken, pltpu.roll(y, 1 << bit, 0), y)
        if step + 1 < STEPS:
            u[step + 1, f] = y
        else:
            obuf[f] = y

    arrive(fields)
    for f in range(AHEAD):
        arrive(f)
    for copy in scalars:
        copy.wait()
    halo_recv(0, fields)
    v, _ = tiles(0, fields)
    speed = 0.5 * (v + back_one(v))
    vn[...] = jnp.minimum(speed, 0.0)
    vp[...] = ahead_one(jnp.maximum(speed, 0.0))

    def work(i):
        @pl.when(i + AHEAD < fields)
        def _():
            arrive(i + AHEAD)

        @pl.when(i < fields)
        def _():
            halo_recv(0, i)
            advance(0, i)
            halo_start(1, i)

        @pl.when(i >= LAG)
        def _():
            halo_recv(1, i - LAG)
            advance(1, i - LAG)
            send_out(i - LAG)

    each(work, fields + LAG)

    def sent(plane):
        all_in(plane).wait_send()
        at_middle = (place == middle - 1) | (place == middle)
        pl.when(at_middle)(cross(plane, 1).wait_send)
        pl.when(jnp.logical_not(at_middle))(cross(plane, 2).wait_send)
        halo_sent(0, plane)

    each(sent, fields + 1)

    def finish(f):
        halo_sent(1, f)
        pltpu.make_async_copy(
            obuf.at[f, rows(me), :], out.at[f, :, lanes(place)], o_own.at[f]
        ).wait()
        others = obuf.at[f, pl.ds(0, azim - block), :]
        done = pltpu.make_async_remote_copy(
            src_ref=others,
            dst_ref=others,
            send_sem=o_send.at[f],
            recv_sem=o_recv.at[f],
            device_id={"azim": outward},
        )
        done.wait_send()
        done.wait_recv()

    each(finish)


def by_radius(conserved, velocity, viscosity, shifts):
    fields, block, cols = conserved.shape
    n = lax.axis_size("azim")
    heights = cols // shifts.shape[1]
    azim = n * block
    f32 = jnp.float32
    dma = pltpu.SemaphoreType.DMA
    operands = (conserved, velocity, viscosity, shifts)
    held = [pltpu.with_memory_space_constraint(x, pltpu.HBM) for x in operands]
    return pl.pallas_call(
        functools.partial(disc_kernel, n, heights),
        out_shape=pltpu.VMEM(conserved.shape, f32),
        in_specs=[pl.BlockSpec(memory_space=pltpu.HBM)] * 4,
        out_specs=pl.BlockSpec(memory_space=pltpu.VMEM),
        scratch_shapes=[
            pltpu.SMEM(viscosity.shape, f32),
            pltpu.SMEM(shifts.shape, jnp.int32),
            dma((2,)),
            pltpu.VMEM((STEPS, fields + 1, azim, LANES), f32),
            pltpu.VMEM((STEPS, fields + 1, azim, LANES), f32),
            pltpu.VMEM((STEPS, fields + 1, azim, LANES), f32),
            pltpu.VMEM((azim, 2 * LANES), f32),
            pltpu.VMEM((azim, 2 * LANES), f32),
            pltpu.VMEM((azim, 2 * LANES), f32),
            pltpu.VMEM((azim, 2 * LANES), f32),
            pltpu.VMEM((3 * LANES, 2 * LANES), jnp.bfloat16),
            pltpu.VMEM((fields, azim, LANES), f32),
            dma((fields + 1,)),
            dma((fields + 1,)),
            dma((fields + 1,)),
            dma((STEPS, 2, fields + 1)),
            dma((STEPS, 2, fields + 1)),
            dma((fields + 1,)),
            dma((fields + 1,)),
            dma((fields + 1,)),
            dma((fields,)),
            dma((fields,)),
            dma((fields,)),
        ],
        compiler_params=pltpu.CompilerParams(
            collective_id=0, has_side_effects=True, vmem_limit_bytes=16 * 1024 * 1024
        ),
    )(*held)


def local(conserved, velocity, viscosity, shifts):
    fields, block, cols = conserved.shape
    n = lax.axis_size("azim")
    heights = cols // shifts.shape[1]
    fits = (
        n == 16
        and n * block == LANES
        and block == SUBLANES
        and cols == n * LANES
        and heights * OWNED == LANES
    )
    if fits:
        return by_radius(conserved, velocity, viscosity, shifts)
    return by_azimuth(conserved, velocity, viscosity, shifts)


def solution(mesh):
    in_specs = (
        P(None, ("groups", "azim"), None),
        P(("groups", "azim"), None),
        P(),
        P("groups", None),
    )
    out_specs = P(None, ("groups", "azim"), None)
    return jax.shard_map(local, mesh=mesh, in_specs=in_specs, out_specs=out_specs, check_vma=False)
```

```python
import functools

import jax
import jax.numpy as jnp
from jax import lax
from jax.experimental import pallas as pl
from jax.experimental.pallas import tpu as pltpu
from jax.sharding import PartitionSpec as P

STEPS = 2
OWNED = 4
LOOK_INNER = 2
LAG = 2
AHEAD = 2
LANES = 128
SUBLANES = 8


def padded(cells, sides, width):
    for axis, dim in sides:
        count = lax.axis_size(axis)
        head = lax.slice_in_dim(cells, 0, width, axis=dim)
        tail = lax.slice_in_dim(cells, cells.shape[dim] - width, cells.shape[dim], axis=dim)
        cells = jnp.concatenate(
            [
                lax.ppermute(tail, axis, [(i, (i + 1) % count) for i in range(count)]),
                cells,
                lax.ppermute(head, axis, [((i + 1) % count, i) for i in range(count)]),
            ],
            axis=dim,
        )
    return cells


def shifted(value, axis, steps):
    count = lax.axis_size(axis)
    pairs = [(source, (source + steps) % count) for source in range(count)]
    return lax.ppermute(value, axis, pairs)


def minmod(left, right):
    return 0.5 * (jnp.sign(left) + jnp.sign(right)) * jnp.minimum(jnp.abs(left), jnp.abs(right))


def lateral_sum(inner, heights):
    width = inner.shape[2]
    height_of = jnp.arange(width, dtype=jnp.int32) % heights
    outward = jnp.concatenate([inner[:, :, heights:], inner[:, :, width - heights :]], axis=2)
    inward = jnp.concatenate([inner[:, :, :heights], inner[:, :, : width - heights]], axis=2)
    upper = jnp.concatenate([inner[:, :, 1:], inner[:, :, width - 1 :]], axis=2)
    upper = jnp.where((height_of == heights - 1)[None, None, :], inner, upper)
    lower = jnp.concatenate([inner[:, :, :1], inner[:, :, : width - 1]], axis=2)
    lower = jnp.where((height_of == 0)[None, None, :], inner, lower)
    return outward + inward + upper + lower - 4.0 * inner


def tendency(ext, speed, viscosity, heights):
    count = ext.shape[1]
    diff = ext[:, 1:] - ext[:, :-1]
    slope = minmod(diff[:, :-1], diff[:, 1:])
    left_state = ext[:, 1 : count - 2] + 0.5 * slope[:, 0 : count - 3]
    right_state = ext[:, 2 : count - 1] - 0.5 * slope[:, 1 : count - 2]
    face_speed = 0.5 * (speed[1 : count - 2] + speed[2 : count - 1])
    flux = jnp.maximum(face_speed, 0.0) * left_state + jnp.minimum(face_speed, 0.0) * right_state
    inner = ext[:, 2 : count - 2]
    azimuthal = ext[:, 3 : count - 1] + ext[:, 1 : count - 3] - 2.0 * inner
    lateral = lateral_sum(inner, heights)
    return -(flux[:, 1:] - flux[:, :-1]) + viscosity[:, None, None] * (azimuthal + lateral)


def section_rim(field):
    return padded(field, (("azim", 1),), 2)


def slide_down(joined, amount, limit):
    current = joined
    level = 0
    while 1 << level < limit:
        stride = 1 << level
        taken = amount >> level & 1 == 1
        moved = jnp.concatenate(
            [jnp.zeros_like(current[:, :stride]), current[:, : current.shape[1] - stride]], axis=1
        )
        current = jnp.where(taken[None, None, :], moved, current)
        level = level + 1
    return current


def by_azimuth(conserved, velocity, viscosity, shifts):
    state = conserved
    block = state.shape[1]
    heights = state.shape[2] // shifts.shape[1]
    devices = lax.axis_size("azim")
    levels = devices.bit_length() - 1
    speed_wide = padded(velocity, (("azim", 0),), 6)
    speed_near = speed_wide[4:-4]
    for step in range(STEPS):
        first = state + tendency(section_rim(state), speed_near, viscosity, heights)
        second = 0.75 * state + 0.25 * (
            first + tendency(section_rim(first), speed_near, viscosity, heights)
        )
        third = 1.0 / 3.0 * state + 2.0 / 3.0 * (
            second + tendency(section_rim(second), speed_near, viscosity, heights)
        )
        per_column = jnp.repeat(shifts[step], heights)
        whole_blocks = per_column // block
        remainder = per_column - whole_blocks * block
        moved = third
        for level in range(levels):
            taken = whole_blocks >> level & 1 == 1
            arrived = shifted(moved, "azim", 1 << level)
            moved = jnp.where(taken[None, None, :], arrived, moved)
        preceding = shifted(moved, "azim", 1)
        joined = jnp.concatenate([preceding, moved], axis=1)
        state = slide_down(joined, remainder, block)[:, block:]
    return state


def winding(d):
    row, chip, core = d // 4, (d % 4) // 2, d % 2
    return row * 4 + ((row + chip) % 2) * 2 + core


def lateral_matrix(place, heights, n):
    total = n * OWNED
    half = OWNED // 2

    def places(axis):
        lane = lax.broadcasted_iota(jnp.int32, (3 * LANES, 2 * LANES), axis)
        height = lane % heights
        group = lane // heights
        tile, slot = group // OWNED, group % OWNED
        inner = jnp.where(slot < half, slot + OWNED, slot - OWNED)
        outer = jnp.where(slot < half, slot - OWNED, slot + OWNED)
        radius = jnp.where(tile == 0, slot, jnp.where(tile == 1, inner, outer))
        return height, radius + place * OWNED

    h_from, r_from = places(0)
    h_to, r_to = places(1)
    inside = (r_from >= 0) & (r_from < total) & (r_to >= 0) & (r_to < total)
    h_gap = jnp.abs(h_from - h_to)
    r_gap = jnp.abs(r_from - r_to)

    def one(condition):
        return jnp.where(condition, 1.0, 0.0)

    own = one(h_to == 0) + one(h_to == heights - 1) + one(r_to == 0) + one(r_to == total - 1) - 4.0
    weight = jnp.where(h_gap + r_gap == 0, own, one(h_gap + r_gap == 1))
    return jnp.where(inside, weight, 0.0).astype(jnp.bfloat16)


def disc_kernel(
    n,
    heights,
    cons,
    vel,
    visc_in,
    shifts_in,
    out,
    visc,
    shifts,
    s_own,
    u,
    mates,
    sides,
    packs,
    vp,
    vn,
    t1,
    t2,
    mat,
    obuf,
    a_send,
    a_recv,
    a_own,
    h_send,
    h_recv,
    x_send,
    x_recv,
    x_own,
    o_send,
    o_recv,
    o_own,
):
    fields, block, cols = cons.shape
    azim = n * block
    me = lax.axis_index("azim")
    place = winding(me)
    odd = lax.rem(place, 2)
    mate = winding(place + 1 - 2 * odd)
    beside = winding(lax.rem(place + n - 1 + 2 * odd, n))
    edge = (place == 0) | (place == n - 1)
    middle = n // 2
    central = (place == middle - 1) | (place == middle)

    barrier = pltpu.get_barrier_semaphore()

    def greet(k, carry):
        pl.semaphore_signal(barrier, inc=1, device_id={"azim": lax.rem(me + k, n)})
        return carry

    lax.fori_loop(1, n, greet, 0)
    pl.semaphore_wait(barrier, n - 1)

    def lanes(d):
        return pl.ds(pl.multiple_of(d * LANES, LANES), LANES)

    def rows(d):
        return pl.ds(pl.multiple_of(d * block, block), block)

    def share(plane, d):
        if isinstance(plane, int) and plane == fields:
            return vel.at[:, lanes(winding(d))]
        return cons.at[plane, :, lanes(winding(d))]

    def send_to(plane, to):
        pltpu.make_async_remote_copy(
            src_ref=share(plane, to),
            dst_ref=u.at[0, plane, rows(me), :],
            send_sem=a_send.at[plane],
            recv_sem=a_recv.at[plane],
            device_id={"azim": to},
        ).start()

    def cross_to(plane, side):
        taker = winding(middle - 1 + side)
        giver = winding(middle - side)
        there = pltpu.make_async_remote_copy(
            src_ref=share(plane, giver),
            dst_ref=sides.at[0, plane, rows(me), :],
            send_sem=x_send.at[plane],
            recv_sem=x_recv.at[plane],
            device_id={"azim": taker},
        )
        here = pltpu.make_async_copy(
            share(plane, giver), sides.at[0, plane, rows(me), :], x_own.at[plane]
        )
        return taker, there, here

    def send_in(plane):
        def one(k, carry):
            send_to(plane, lax.rem(me + k, n))
            return carry

        lax.fori_loop(1, n, one, 0)
        pltpu.make_async_copy(
            share(plane, me), u.at[0, plane, rows(me), :], a_own.at[plane]
        ).start()
        for side in (0, 1):
            taker, there, here = cross_to(plane, side)
            pl.when(taker != me)(there.start)
            pl.when(taker == me)(here.start)

    def send_at(f, carry):
        send_in(f)
        return carry

    row = me // 4
    inside = (row > 0) & (row < n // 4 - 1)
    early = jnp.where(inside, LOOK_INNER, fields)
    send_in(fields)
    lax.fori_loop(0, early, send_at, 0)

    scalars = (
        pltpu.make_async_copy(visc_in, visc, s_own.at[0]),
        pltpu.make_async_copy(shifts_in, shifts, s_own.at[1]),
    )
    for copy in scalars:
        copy.start()

    def all_in(plane):
        others = u.at[0, plane, pl.ds(0, azim - block), :]
        return pltpu.make_async_remote_copy(
            src_ref=others,
            dst_ref=others,
            send_sem=a_send.at[plane],
            recv_sem=a_recv.at[plane],
            device_id={"azim": mate},
        )

    def cross(plane, count):
        others = sides.at[0, plane, pl.ds(0, count * block), :]
        return pltpu.make_async_remote_copy(
            src_ref=others,
            dst_ref=others,
            send_sem=x_send.at[plane],
            recv_sem=x_recv.at[plane],
            device_id={"azim": mate},
        )

    held = azim // OWNED
    lane = lax.broadcasted_iota(jnp.int32, (azim, LANES), 1)
    lower = (lane < LANES // 2) == (odd == 0)
    spare = lane[:held] // heights == jnp.where(odd == 0, OWNED - 1, 0)

    def pack(step, plane):
        last = u[step, plane, azim - held :, :]
        for j in range(OWNED - 1):
            moved = pltpu.roll(last, LANES - (j + 1) * heights, 1)
            part = slice(j * held, (j + 1) * held)
            packs[step, plane, part, :] = jnp.where(spare, moved, u[step, plane, part, :])

    def unpack(step, plane):
        last = jnp.zeros((held, LANES), jnp.float32)
        for j in range(OWNED - 1):
            moved = pltpu.roll(sides[step, plane, j * held : (j + 1) * held, :], (j + 1) * heights, 1)
            here = lane[:held] // heights == j + 1 - odd
            last = jnp.where(here, moved, last)
        sides[step, plane, azim - held :, :] = last

    def across(step):
        return jnp.logical_not(edge | central) if step == 0 else jnp.logical_not(edge)

    def halo(step, plane):
        near = pltpu.make_async_remote_copy(
            src_ref=u.at[step, plane],
            dst_ref=mates.at[step, plane],
            send_sem=h_send.at[step, 0, plane],
            recv_sem=h_recv.at[step, 0, plane],
            device_id={"azim": mate},
        )
        far = pltpu.make_async_remote_copy(
            src_ref=packs.at[step, plane],
            dst_ref=sides.at[step, plane, pl.ds(0, azim - held), :],
            send_sem=h_send.at[step, 1, plane],
            recv_sem=h_recv.at[step, 1, plane],
            device_id={"azim": beside},
        )
        return near, far

    def halo_start(step, plane):
        near, far = halo(step, plane)

        @pl.when(across(step))
        def _():
            pack(step, plane)
            far.start()

        near.start()

    def halo_recv(step, plane):
        near, far = halo(step, plane)
        near.wait_recv()

        @pl.when(across(step))
        def _():
            far.wait_recv()
            unpack(step, plane)

        if step == 0:

            @pl.when(central)
            def _():
                own = sides.at[0, plane, rows(me), :]
                pltpu.make_async_copy(own, own, x_own.at[plane]).wait()
                cross(plane, n - 1).wait_recv()

    def halo_sent(step, plane):
        near, far = halo(step, plane)
        near.wait_send()
        pl.when(across(step))(far.wait_send)

    def arrive(plane):
        pltpu.make_async_copy(
            u.at[0, plane, rows(me), :], u.at[0, plane, rows(me), :], a_own.at[plane]
        ).wait()
        all_in(plane).wait_recv()
        halo_start(0, plane)
        later = early if isinstance(plane, int) and plane == fields else plane + early + 1
        pl.when(later < fields)(lambda: send_in(later))

    def send_out(f):
        def one(to, carry):
            @pl.when(to != me)
            def _():
                pltpu.make_async_remote_copy(
                    src_ref=obuf.at[f, rows(to), :],
                    dst_ref=out.at[f, :, lanes(place)],
                    send_sem=o_send.at[f],
                    recv_sem=o_recv.at[f],
                    device_id={"azim": to},
                ).start()

            return carry

        lax.fori_loop(0, n, one, 0)
        pltpu.make_async_copy(obuf.at[f, rows(me), :], out.at[f, :, lanes(place)], o_own.at[f]).start()

    def each(body, count=fields):
        def one(f, carry):
            body(f)
            return carry

        lax.fori_loop(0, count, one, 0)

    def clear(tile):
        def one(plane, carry):
            for step in range(STEPS):
                tile[step, plane] = jnp.zeros((azim, LANES), jnp.float32)
            return carry

        lax.fori_loop(0, fields + 1, one, 0)

    pl.when(edge)(lambda: clear(sides))
    mat[...] = lateral_matrix(place, heights, n)

    def tiles(step, plane):
        own, close, side = u[step, plane], mates[step, plane], sides[step, plane]
        near = jnp.concatenate([own, jnp.where(lower, close, side)], axis=1)
        return near, jnp.where(lower, side, close)

    def ahead_one(x):
        return pltpu.roll(x, azim - 1, 0)

    def back_one(x):
        return pltpu.roll(x, 1, 0)

    def halves(x):
        high = x.astype(jnp.bfloat16)
        return high, (x - high.astype(jnp.float32)).astype(jnp.bfloat16)

    def lateral(x, count):
        both = jnp.concatenate(halves(x), axis=0)
        y = jnp.dot(both, mat[: 2 * LANES, :count], preferred_element_type=jnp.float32)
        return y[:azim] + y[azim:]

    def change(x, spread, nu):
        count = spread.shape[1]
        x = x[:, :count]
        d = x - back_one(x)
        dp = ahead_one(d)
        low = jnp.minimum(d, dp)
        high = jnp.maximum(d, dp)
        half = 0.5 * (jnp.maximum(low, 0.0) + jnp.minimum(high, 0.0))
        p = vp[:, :count] * (x + half)
        q = vn[:, :count] * (x - half)
        flow = (p - q) + (ahead_one(q) - back_one(p))
        return x + (nu * ((dp - d) + spread) - flow)

    def advance(step, f):
        nu = visc[f]
        near, far = tiles(step, f)
        rim = mat[2 * LANES :, :]
        spread = lateral(near, 2 * LANES) + jnp.dot(
            jnp.concatenate(halves(far), axis=1),
            jnp.concatenate([rim, rim], axis=0),
            preferred_element_type=jnp.float32,
        )
        t1[...] = change(near, spread, nu)
        x = t1[...]
        t2[...] = 0.75 * near + 0.25 * change(x, lateral(x, 2 * LANES), nu)
        x = t2[...]
        y = (1.0 / 3.0) * near[:, :LANES] + (2.0 / 3.0) * change(x, lateral(x, LANES), nu)
        slot = lax.broadcasted_iota(jnp.int32, (SUBLANES, LANES), 1) // heights
        amount = jnp.zeros((SUBLANES, LANES), jnp.int32)
        for r in range(OWNED):
            amount = jnp.where(slot == r, shifts[step, place * OWNED + r], amount)
        for bit in range(azim.bit_length() - 1):
            taken = ((amount >> bit) & 1 == 1)[:1]
            taken = jnp.broadcast_to(taken, (azim, LANES))
            y = jnp.where(taken, pltpu.roll(y, 1 << bit, 0), y)
        if step + 1 < STEPS:
            u[step + 1, f] = y
        else:
            obuf[f] = y

    arrive(fields)
    for f in range(AHEAD):
        arrive(f)
    for copy in scalars:
        copy.wait()
    halo_recv(0, fields)
    v, _ = tiles(0, fields)
    speed = 0.5 * (v + back_one(v))
    vn[...] = jnp.minimum(speed, 0.0)
    vp[...] = ahead_one(jnp.maximum(speed, 0.0))

    def work(i):
        @pl.when(i + AHEAD < fields)
        def _():
            arrive(i + AHEAD)

        @pl.when(i < fields)
        def _():
            halo_recv(0, i)
            advance(0, i)
            halo_start(1, i)

        @pl.when(i >= LAG)
        def _():
            halo_recv(1, i - LAG)
            advance(1, i - LAG)
            send_out(i - LAG)

    each(work, fields + LAG)

    def sent(plane):
        all_in(plane).wait_send()
        pl.when(central)(cross(plane, 1).wait_send)
        pl.when(jnp.logical_not(central))(cross(plane, 2).wait_send)
        halo_sent(0, plane)

    each(sent, fields + 1)

    def finish(f):
        halo_sent(1, f)
        pltpu.make_async_copy(
            obuf.at[f, rows(me), :], out.at[f, :, lanes(place)], o_own.at[f]
        ).wait()
        others = obuf.at[f, pl.ds(0, azim - block), :]
        done = pltpu.make_async_remote_copy(
            src_ref=others,
            dst_ref=others,
            send_sem=o_send.at[f],
            recv_sem=o_recv.at[f],
            device_id={"azim": mate},
        )
        done.wait_send()
        done.wait_recv()

    each(finish)


def by_radius(conserved, velocity, viscosity, shifts):
    fields, block, cols = conserved.shape
    n = lax.axis_size("azim")
    heights = cols // shifts.shape[1]
    azim = n * block
    f32 = jnp.float32
    dma = pltpu.SemaphoreType.DMA
    operands = (conserved, velocity, viscosity, shifts)
    held = [pltpu.with_memory_space_constraint(x, pltpu.HBM) for x in operands]
    return pl.pallas_call(
        functools.partial(disc_kernel, n, heights),
        out_shape=pltpu.VMEM(conserved.shape, f32),
        in_specs=[pl.BlockSpec(memory_space=pltpu.HBM)] * 4,
        out_specs=pl.BlockSpec(memory_space=pltpu.VMEM),
        scratch_shapes=[
            pltpu.SMEM(viscosity.shape, f32),
            pltpu.SMEM(shifts.shape, jnp.int32),
            dma((2,)),
            pltpu.VMEM((STEPS, fields + 1, azim, LANES), f32),
            pltpu.VMEM((STEPS, fields + 1, azim, LANES), f32),
            pltpu.VMEM((STEPS, fields + 1, azim, LANES), f32),
            pltpu.VMEM((STEPS, fields + 1, azim - azim // OWNED, LANES), f32),
            pltpu.VMEM((azim, 2 * LANES), f32),
            pltpu.VMEM((azim, 2 * LANES), f32),
            pltpu.VMEM((azim, 2 * LANES), f32),
            pltpu.VMEM((azim, 2 * LANES), f32),
            pltpu.VMEM((3 * LANES, 2 * LANES), jnp.bfloat16),
            pltpu.VMEM((fields, azim, LANES), f32),
            dma((fields + 1,)),
            dma((fields + 1,)),
            dma((fields + 1,)),
            dma((STEPS, 2, fields + 1)),
            dma((STEPS, 2, fields + 1)),
            dma((fields + 1,)),
            dma((fields + 1,)),
            dma((fields + 1,)),
            dma((fields,)),
            dma((fields,)),
            dma((fields,)),
        ],
        compiler_params=pltpu.CompilerParams(
            collective_id=0, has_side_effects=True, vmem_limit_bytes=16 * 1024 * 1024
        ),
    )(*held)


def local(conserved, velocity, viscosity, shifts):
    fields, block, cols = conserved.shape
    n = lax.axis_size("azim")
    heights = cols // shifts.shape[1]
    fits = (
        n == 16
        and n * block == LANES
        and block == SUBLANES
        and cols == n * LANES
        and heights * OWNED == LANES
    )
    if fits:
        return by_radius(conserved, velocity, viscosity, shifts)
    return by_azimuth(conserved, velocity, viscosity, shifts)


def solution(mesh):
    in_specs = (
        P(None, ("groups", "azim"), None),
        P(("groups", "azim"), None),
        P(),
        P("groups", None),
    )
    out_specs = P(None, ("groups", "azim"), None)
    return jax.shard_map(local, mesh=mesh, in_specs=in_specs, out_specs=out_specs, check_vma=False)
```

```python
import functools

import jax
import jax.numpy as jnp
from jax import lax
from jax.experimental import pallas as pl
from jax.experimental.pallas import tpu as pltpu
from jax.sharding import PartitionSpec as P

STEPS = 2
OWNED = 4
LOOK_INNER = 2
LAG = 2
AHEAD = 2
LANES = 128
SUBLANES = 8


def padded(cells, sides, width):
    for axis, dim in sides:
        count = lax.axis_size(axis)
        head = lax.slice_in_dim(cells, 0, width, axis=dim)
        tail = lax.slice_in_dim(cells, cells.shape[dim] - width, cells.shape[dim], axis=dim)
        cells = jnp.concatenate(
            [
                lax.ppermute(tail, axis, [(i, (i + 1) % count) for i in range(count)]),
                cells,
                lax.ppermute(head, axis, [((i + 1) % count, i) for i in range(count)]),
            ],
            axis=dim,
        )
    return cells


def shifted(value, axis, steps):
    count = lax.axis_size(axis)
    pairs = [(source, (source + steps) % count) for source in range(count)]
    return lax.ppermute(value, axis, pairs)


def minmod(left, right):
    return 0.5 * (jnp.sign(left) + jnp.sign(right)) * jnp.minimum(jnp.abs(left), jnp.abs(right))


def lateral_sum(inner, heights):
    width = inner.shape[2]
    height_of = jnp.arange(width, dtype=jnp.int32) % heights
    outward = jnp.concatenate([inner[:, :, heights:], inner[:, :, width - heights :]], axis=2)
    inward = jnp.concatenate([inner[:, :, :heights], inner[:, :, : width - heights]], axis=2)
    upper = jnp.concatenate([inner[:, :, 1:], inner[:, :, width - 1 :]], axis=2)
    upper = jnp.where((height_of == heights - 1)[None, None, :], inner, upper)
    lower = jnp.concatenate([inner[:, :, :1], inner[:, :, : width - 1]], axis=2)
    lower = jnp.where((height_of == 0)[None, None, :], inner, lower)
    return outward + inward + upper + lower - 4.0 * inner


def tendency(ext, speed, viscosity, heights):
    count = ext.shape[1]
    diff = ext[:, 1:] - ext[:, :-1]
    slope = minmod(diff[:, :-1], diff[:, 1:])
    left_state = ext[:, 1 : count - 2] + 0.5 * slope[:, 0 : count - 3]
    right_state = ext[:, 2 : count - 1] - 0.5 * slope[:, 1 : count - 2]
    face_speed = 0.5 * (speed[1 : count - 2] + speed[2 : count - 1])
    flux = jnp.maximum(face_speed, 0.0) * left_state + jnp.minimum(face_speed, 0.0) * right_state
    inner = ext[:, 2 : count - 2]
    azimuthal = ext[:, 3 : count - 1] + ext[:, 1 : count - 3] - 2.0 * inner
    lateral = lateral_sum(inner, heights)
    return -(flux[:, 1:] - flux[:, :-1]) + viscosity[:, None, None] * (azimuthal + lateral)


def section_rim(field):
    return padded(field, (("azim", 1),), 2)


def slide_down(joined, amount, limit):
    current = joined
    level = 0
    while 1 << level < limit:
        stride = 1 << level
        taken = amount >> level & 1 == 1
        moved = jnp.concatenate(
            [jnp.zeros_like(current[:, :stride]), current[:, : current.shape[1] - stride]], axis=1
        )
        current = jnp.where(taken[None, None, :], moved, current)
        level = level + 1
    return current


def by_azimuth(conserved, velocity, viscosity, shifts):
    state = conserved
    block = state.shape[1]
    heights = state.shape[2] // shifts.shape[1]
    devices = lax.axis_size("azim")
    levels = devices.bit_length() - 1
    speed_wide = padded(velocity, (("azim", 0),), 6)
    speed_near = speed_wide[4:-4]
    for step in range(STEPS):
        first = state + tendency(section_rim(state), speed_near, viscosity, heights)
        second = 0.75 * state + 0.25 * (
            first + tendency(section_rim(first), speed_near, viscosity, heights)
        )
        third = 1.0 / 3.0 * state + 2.0 / 3.0 * (
            second + tendency(section_rim(second), speed_near, viscosity, heights)
        )
        per_column = jnp.repeat(shifts[step], heights)
        whole_blocks = per_column // block
        remainder = per_column - whole_blocks * block
        moved = third
        for level in range(levels):
            taken = whole_blocks >> level & 1 == 1
            arrived = shifted(moved, "azim", 1 << level)
            moved = jnp.where(taken[None, None, :], arrived, moved)
        preceding = shifted(moved, "azim", 1)
        joined = jnp.concatenate([preceding, moved], axis=1)
        state = slide_down(joined, remainder, block)[:, block:]
    return state


def winding(d):
    row, chip, core = d // 4, (d % 4) // 2, d % 2
    return row * 4 + ((row + chip) % 2) * 2 + core


def lateral_matrix(place, heights, n):
    total = n * OWNED
    half = OWNED // 2

    def places(axis):
        lane = lax.broadcasted_iota(jnp.int32, (3 * LANES, 2 * LANES), axis)
        height = lane % heights
        group = lane // heights
        tile, slot = group // OWNED, group % OWNED
        inner = jnp.where(slot < half, slot + OWNED, slot - OWNED)
        outer = jnp.where(slot < half, slot - OWNED, slot + OWNED)
        radius = jnp.where(tile == 0, slot, jnp.where(tile == 1, inner, outer))
        return height, radius + place * OWNED

    h_from, r_from = places(0)
    h_to, r_to = places(1)
    inside = (r_from >= 0) & (r_from < total) & (r_to >= 0) & (r_to < total)
    h_gap = jnp.abs(h_from - h_to)
    r_gap = jnp.abs(r_from - r_to)

    def one(condition):
        return jnp.where(condition, 1.0, 0.0)

    own = one(h_to == 0) + one(h_to == heights - 1) + one(r_to == 0) + one(r_to == total - 1) - 4.0
    weight = jnp.where(h_gap + r_gap == 0, own, one(h_gap + r_gap == 1))
    return jnp.where(inside, weight, 0.0).astype(jnp.bfloat16)


def disc_kernel(
    n,
    heights,
    cons,
    vel,
    visc_in,
    shifts_in,
    out,
    visc,
    shifts,
    s_own,
    u,
    mates,
    sides,
    packs,
    vp,
    vn,
    t1,
    t2,
    mat,
    obuf,
    a_send,
    a_recv,
    a_own,
    h_send,
    h_recv,
    x_send,
    x_recv,
    x_own,
    o_send,
    o_recv,
    o_own,
):
    fields, block, cols = cons.shape
    azim = n * block
    me = lax.axis_index("azim")
    place = winding(me)
    odd = lax.rem(place, 2)
    mate = winding(place + 1 - 2 * odd)
    beside = winding(lax.rem(place + n - 1 + 2 * odd, n))
    edge = (place == 0) | (place == n - 1)
    middle = n // 2
    central = (place == middle - 1) | (place == middle)

    barrier = pltpu.get_barrier_semaphore()

    def greet(k, carry):
        pl.semaphore_signal(barrier, inc=1, device_id={"azim": lax.rem(me + k, n)})
        return carry

    lax.fori_loop(1, n, greet, 0)
    pl.semaphore_wait(barrier, n - 1)

    def lanes(d):
        return pl.ds(pl.multiple_of(d * LANES, LANES), LANES)

    def rows(d):
        return pl.ds(pl.multiple_of(d * block, block), block)

    def share(plane, d):
        if isinstance(plane, int) and plane == fields:
            return vel.at[:, lanes(winding(d))]
        return cons.at[plane, :, lanes(winding(d))]

    def send_to(plane, to):
        pltpu.make_async_remote_copy(
            src_ref=share(plane, to),
            dst_ref=u.at[0, plane, rows(me), :],
            send_sem=a_send.at[plane],
            recv_sem=a_recv.at[plane],
            device_id={"azim": to},
        ).start()

    def cross_to(plane, side):
        taker = winding(middle - 1 + side)
        giver = winding(middle - side)
        there = pltpu.make_async_remote_copy(
            src_ref=share(plane, giver),
            dst_ref=sides.at[0, plane, rows(me), :],
            send_sem=x_send.at[plane],
            recv_sem=x_recv.at[plane],
            device_id={"azim": taker},
        )
        here = pltpu.make_async_copy(
            share(plane, giver), sides.at[0, plane, rows(me), :], x_own.at[plane]
        )
        return taker, there, here

    def send_in(plane):
        def one(k, carry):
            send_to(plane, lax.rem(me + k, n))
            return carry

        lax.fori_loop(1, n, one, 0)
        pltpu.make_async_copy(
            share(plane, me), u.at[0, plane, rows(me), :], a_own.at[plane]
        ).start()
        for side in (0, 1):
            taker, there, here = cross_to(plane, side)
            pl.when(taker != me)(there.start)
            pl.when(taker == me)(here.start)

    def send_at(f, carry):
        send_in(f)
        return carry

    row = me // 4
    inside = (row > 0) & (row < n // 4 - 1)
    early = jnp.where(inside, LOOK_INNER, fields)
    send_in(fields)
    lax.fori_loop(0, early, send_at, 0)

    scalars = (
        pltpu.make_async_copy(visc_in, visc, s_own.at[0]),
        pltpu.make_async_copy(shifts_in, shifts, s_own.at[1]),
    )
    for copy in scalars:
        copy.start()

    def all_in(plane):
        others = u.at[0, plane, pl.ds(0, azim - block), :]
        return pltpu.make_async_remote_copy(
            src_ref=others,
            dst_ref=others,
            send_sem=a_send.at[plane],
            recv_sem=a_recv.at[plane],
            device_id={"azim": mate},
        )

    def cross(plane, count):
        others = sides.at[0, plane, pl.ds(0, count * block), :]
        return pltpu.make_async_remote_copy(
            src_ref=others,
            dst_ref=others,
            send_sem=x_send.at[plane],
            recv_sem=x_recv.at[plane],
            device_id={"azim": mate},
        )

    held = azim // OWNED
    lane = lax.broadcasted_iota(jnp.int32, (azim, LANES), 1)
    lower = (lane < LANES // 2) == (odd == 0)
    spare = lane[:held] // heights == jnp.where(odd == 0, OWNED - 1, 0)

    def pack(step, plane):
        last = u[step, plane, azim - held :, :]
        for j in range(OWNED - 1):
            moved = pltpu.roll(last, LANES - (j + 1) * heights, 1)
            part = slice(j * held, (j + 1) * held)
            packs[step, plane, part, :] = jnp.where(spare, moved, u[step, plane, part, :])

    def unpack(step, plane):
        last = jnp.zeros((held, LANES), jnp.float32)
        for j in range(OWNED - 1):
            moved = pltpu.roll(sides[step, plane, j * held : (j + 1) * held, :], (j + 1) * heights, 1)
            here = lane[:held] // heights == j + 1 - odd
            last = jnp.where(here, moved, last)
        sides[step, plane, azim - held :, :] = last

    def across(step):
        return jnp.logical_not(edge | central) if step == 0 else jnp.logical_not(edge)

    def halo(step, plane):
        near = pltpu.make_async_remote_copy(
            src_ref=u.at[step, plane],
            dst_ref=mates.at[step, plane],
            send_sem=h_send.at[step, 0, plane],
            recv_sem=h_recv.at[step, 0, plane],
            device_id={"azim": mate},
        )
        far = pltpu.make_async_remote_copy(
            src_ref=packs.at[step, plane],
            dst_ref=sides.at[step, plane, pl.ds(0, azim - held), :],
            send_sem=h_send.at[step, 1, plane],
            recv_sem=h_recv.at[step, 1, plane],
            device_id={"azim": beside},
        )
        return near, far

    def halo_start(step, plane):
        near, far = halo(step, plane)
        near.start()

        @pl.when(across(step))
        def _():
            pack(step, plane)
            far.start()


    def halo_recv(step, plane):
        near, far = halo(step, plane)
        near.wait_recv()

        @pl.when(across(step))
        def _():
            far.wait_recv()
            unpack(step, plane)

        if step == 0:

            @pl.when(central)
            def _():
                own = sides.at[0, plane, rows(me), :]
                pltpu.make_async_copy(own, own, x_own.at[plane]).wait()
                cross(plane, n - 1).wait_recv()

    def halo_sent(step, plane):
        near, far = halo(step, plane)
        near.wait_send()
        pl.when(across(step))(far.wait_send)

    def arrive(plane):
        pltpu.make_async_copy(
            u.at[0, plane, rows(me), :], u.at[0, plane, rows(me), :], a_own.at[plane]
        ).wait()
        all_in(plane).wait_recv()
        halo_start(0, plane)
        later = early if isinstance(plane, int) and plane == fields else plane + early + 1
        pl.when(later < fields)(lambda: send_in(later))

    def send_out(f):
        def one(to, carry):
            @pl.when(to != me)
            def _():
                pltpu.make_async_remote_copy(
                    src_ref=obuf.at[f, rows(to), :],
                    dst_ref=out.at[f, :, lanes(place)],
                    send_sem=o_send.at[f],
                    recv_sem=o_recv.at[f],
                    device_id={"azim": to},
                ).start()

            return carry

        lax.fori_loop(0, n, one, 0)

    def own_out(f):
        return pltpu.make_async_copy(
            obuf.at[f, rows(me), :], out.at[f, :, lanes(place)], o_own.at[f]
        )

    def each(body, count=fields):
        def one(f, carry):
            body(f)
            return carry

        lax.fori_loop(0, count, one, 0)

    def clear(tile):
        def one(plane, carry):
            for step in range(STEPS):
                tile[step, plane] = jnp.zeros((azim, LANES), jnp.float32)
            return carry

        lax.fori_loop(0, fields + 1, one, 0)

    pl.when(edge)(lambda: clear(sides))
    mat[...] = lateral_matrix(place, heights, n)

    def tiles(step, plane):
        own, close, side = u[step, plane], mates[step, plane], sides[step, plane]
        near = jnp.concatenate([own, jnp.where(lower, close, side)], axis=1)
        return near, jnp.where(lower, side, close)

    def ahead_one(x):
        return pltpu.roll(x, azim - 1, 0)

    def back_one(x):
        return pltpu.roll(x, 1, 0)

    def halves(x):
        high = x.astype(jnp.bfloat16)
        return high, (x - high.astype(jnp.float32)).astype(jnp.bfloat16)

    def lateral(x, count):
        parts = []
        size = azim // 2
        for k in range(2):
            both = jnp.concatenate(halves(x[k * size : (k + 1) * size]), axis=0)
            y = jnp.dot(both, mat[: 2 * LANES, :count], preferred_element_type=jnp.float32)
            parts.append(y[:size] + y[size:])
        return jnp.concatenate(parts, axis=0)

    def change(x, spread, nu):
        count = spread.shape[1]
        x = x[:, :count]
        d = x - back_one(x)
        dp = ahead_one(d)
        low = jnp.minimum(d, dp)
        high = jnp.maximum(d, dp)
        half = 0.5 * (jnp.maximum(low, 0.0) + jnp.minimum(high, 0.0))
        p = vp[:, :count] * (x + half)
        q = vn[:, :count] * (x - half)
        flow = (p - q) + (ahead_one(q) - back_one(p))
        return x + (nu * ((dp - d) + spread) - flow)

    def advance(step, f):
        nu = visc[f]
        near, far = tiles(step, f)
        rim = mat[2 * LANES :, :]
        spread = lateral(near, 2 * LANES) + jnp.dot(
            jnp.concatenate(halves(far), axis=1),
            jnp.concatenate([rim, rim], axis=0),
            preferred_element_type=jnp.float32,
        )
        t1[...] = change(near, spread, nu)
        x = t1[...]
        t2[...] = 0.75 * near + 0.25 * change(x, lateral(x, 2 * LANES), nu)
        x = t2[...]
        y = (1.0 / 3.0) * near[:, :LANES] + (2.0 / 3.0) * change(x, lateral(x, LANES), nu)
        slot = lax.broadcasted_iota(jnp.int32, (SUBLANES, LANES), 1) // heights
        amount = jnp.zeros((SUBLANES, LANES), jnp.int32)
        for r in range(OWNED):
            amount = jnp.where(slot == r, shifts[step, place * OWNED + r], amount)
        for bit in range(azim.bit_length() - 1):
            taken = ((amount >> bit) & 1 == 1)[:1]
            taken = jnp.broadcast_to(taken, (azim, LANES))
            y = jnp.where(taken, pltpu.roll(y, 1 << bit, 0), y)
        if step + 1 < STEPS:
            u[step + 1, f] = y
        else:
            obuf[f] = y

    arrive(fields)
    for f in range(AHEAD):
        arrive(f)
    for copy in scalars:
        copy.wait()
    halo_recv(0, fields)
    v, _ = tiles(0, fields)
    speed = 0.5 * (v + back_one(v))
    vn[...] = jnp.minimum(speed, 0.0)
    vp[...] = ahead_one(jnp.maximum(speed, 0.0))

    def work(i):
        @pl.when(i + AHEAD < fields)
        def _():
            arrive(i + AHEAD)

        @pl.when(i < fields)
        def _():
            halo_recv(0, i)
            advance(0, i)
            halo_start(1, i)

        @pl.when(i >= LAG)
        def _():
            halo_recv(1, i - LAG)
            advance(1, i - LAG)
            own_out(i - LAG).start()
            send_out(i - LAG)

    each(work, fields + LAG)

    def sent(plane):
        all_in(plane).wait_send()
        pl.when(central)(cross(plane, 1).wait_send)
        pl.when(jnp.logical_not(central))(cross(plane, 2).wait_send)
        halo_sent(0, plane)

    each(sent, fields + 1)

    def finish(f):
        halo_sent(1, f)
        own_out(f).wait()
        others = obuf.at[f, pl.ds(0, azim - block), :]
        done = pltpu.make_async_remote_copy(
            src_ref=others,
            dst_ref=others,
            send_sem=o_send.at[f],
            recv_sem=o_recv.at[f],
            device_id={"azim": mate},
        )
        done.wait_send()
        done.wait_recv()

    each(finish)


def by_radius(conserved, velocity, viscosity, shifts):
    fields, block, cols = conserved.shape
    n = lax.axis_size("azim")
    heights = cols // shifts.shape[1]
    azim = n * block
    f32 = jnp.float32
    dma = pltpu.SemaphoreType.DMA
    operands = (conserved, velocity, viscosity, shifts)
    held = [pltpu.with_memory_space_constraint(x, pltpu.HBM) for x in operands]
    return pl.pallas_call(
        functools.partial(disc_kernel, n, heights),
        out_shape=pltpu.VMEM(conserved.shape, f32),
        in_specs=[pl.BlockSpec(memory_space=pltpu.HBM)] * 4,
        out_specs=pl.BlockSpec(memory_space=pltpu.VMEM),
        scratch_shapes=[
            pltpu.SMEM(viscosity.shape, f32),
            pltpu.SMEM(shifts.shape, jnp.int32),
            dma((2,)),
            pltpu.VMEM((STEPS, fields + 1, azim, LANES), f32),
            pltpu.VMEM((STEPS, fields + 1, azim, LANES), f32),
            pltpu.VMEM((STEPS, fields + 1, azim, LANES), f32),
            pltpu.VMEM((STEPS, fields + 1, azim - azim // OWNED, LANES), f32),
            pltpu.VMEM((azim, 2 * LANES), f32),
            pltpu.VMEM((azim, 2 * LANES), f32),
            pltpu.VMEM((azim, 2 * LANES), f32),
            pltpu.VMEM((azim, 2 * LANES), f32),
            pltpu.VMEM((3 * LANES, 2 * LANES), jnp.bfloat16),
            pltpu.VMEM((fields, azim, LANES), f32),
            dma((fields + 1,)),
            dma((fields + 1,)),
            dma((fields + 1,)),
            dma((STEPS, 2, fields + 1)),
            dma((STEPS, 2, fields + 1)),
            dma((fields + 1,)),
            dma((fields + 1,)),
            dma((fields + 1,)),
            dma((fields,)),
            dma((fields,)),
            dma((fields,)),
        ],
        compiler_params=pltpu.CompilerParams(
            collective_id=0, has_side_effects=True, vmem_limit_bytes=16 * 1024 * 1024
        ),
    )(*held)


def local(conserved, velocity, viscosity, shifts):
    fields, block, cols = conserved.shape
    n = lax.axis_size("azim")
    heights = cols // shifts.shape[1]
    fits = (
        n == 16
        and n * block == LANES
        and block == SUBLANES
        and cols == n * LANES
        and heights * OWNED == LANES
    )
    if fits:
        return by_radius(conserved, velocity, viscosity, shifts)
    return by_azimuth(conserved, velocity, viscosity, shifts)


def solution(mesh):
    in_specs = (
        P(None, ("groups", "azim"), None),
        P(("groups", "azim"), None),
        P(),
        P("groups", None),
    )
    out_specs = P(None, ("groups", "azim"), None)
    return jax.shard_map(local, mesh=mesh, in_specs=in_specs, out_specs=out_specs, check_vma=False)
```

```python
import functools

import jax
import jax.numpy as jnp
from jax import lax
from jax.experimental import pallas as pl
from jax.experimental.pallas import tpu as pltpu
from jax.sharding import PartitionSpec as P

STEPS = 2
OWNED = 4
LOOK_INNER = 2
LAG = 2
AHEAD = 2
LANES = 128
SUBLANES = 8


def padded(cells, sides, width):
    for axis, dim in sides:
        count = lax.axis_size(axis)
        head = lax.slice_in_dim(cells, 0, width, axis=dim)
        tail = lax.slice_in_dim(cells, cells.shape[dim] - width, cells.shape[dim], axis=dim)
        cells = jnp.concatenate(
            [
                lax.ppermute(tail, axis, [(i, (i + 1) % count) for i in range(count)]),
                cells,
                lax.ppermute(head, axis, [((i + 1) % count, i) for i in range(count)]),
            ],
            axis=dim,
        )
    return cells


def shifted(value, axis, steps):
    count = lax.axis_size(axis)
    pairs = [(source, (source + steps) % count) for source in range(count)]
    return lax.ppermute(value, axis, pairs)


def minmod(left, right):
    return 0.5 * (jnp.sign(left) + jnp.sign(right)) * jnp.minimum(jnp.abs(left), jnp.abs(right))


def lateral_sum(inner, heights):
    width = inner.shape[2]
    height_of = jnp.arange(width, dtype=jnp.int32) % heights
    outward = jnp.concatenate([inner[:, :, heights:], inner[:, :, width - heights :]], axis=2)
    inward = jnp.concatenate([inner[:, :, :heights], inner[:, :, : width - heights]], axis=2)
    upper = jnp.concatenate([inner[:, :, 1:], inner[:, :, width - 1 :]], axis=2)
    upper = jnp.where((height_of == heights - 1)[None, None, :], inner, upper)
    lower = jnp.concatenate([inner[:, :, :1], inner[:, :, : width - 1]], axis=2)
    lower = jnp.where((height_of == 0)[None, None, :], inner, lower)
    return outward + inward + upper + lower - 4.0 * inner


def tendency(ext, speed, viscosity, heights):
    count = ext.shape[1]
    diff = ext[:, 1:] - ext[:, :-1]
    slope = minmod(diff[:, :-1], diff[:, 1:])
    left_state = ext[:, 1 : count - 2] + 0.5 * slope[:, 0 : count - 3]
    right_state = ext[:, 2 : count - 1] - 0.5 * slope[:, 1 : count - 2]
    face_speed = 0.5 * (speed[1 : count - 2] + speed[2 : count - 1])
    flux = jnp.maximum(face_speed, 0.0) * left_state + jnp.minimum(face_speed, 0.0) * right_state
    inner = ext[:, 2 : count - 2]
    azimuthal = ext[:, 3 : count - 1] + ext[:, 1 : count - 3] - 2.0 * inner
    lateral = lateral_sum(inner, heights)
    return -(flux[:, 1:] - flux[:, :-1]) + viscosity[:, None, None] * (azimuthal + lateral)


def section_rim(field):
    return padded(field, (("azim", 1),), 2)


def slide_down(joined, amount, limit):
    current = joined
    level = 0
    while 1 << level < limit:
        stride = 1 << level
        taken = amount >> level & 1 == 1
        moved = jnp.concatenate(
            [jnp.zeros_like(current[:, :stride]), current[:, : current.shape[1] - stride]], axis=1
        )
        current = jnp.where(taken[None, None, :], moved, current)
        level = level + 1
    return current


def by_azimuth(conserved, velocity, viscosity, shifts):
    state = conserved
    block = state.shape[1]
    heights = state.shape[2] // shifts.shape[1]
    devices = lax.axis_size("azim")
    levels = devices.bit_length() - 1
    speed_wide = padded(velocity, (("azim", 0),), 6)
    speed_near = speed_wide[4:-4]
    for step in range(STEPS):
        first = state + tendency(section_rim(state), speed_near, viscosity, heights)
        second = 0.75 * state + 0.25 * (
            first + tendency(section_rim(first), speed_near, viscosity, heights)
        )
        third = 1.0 / 3.0 * state + 2.0 / 3.0 * (
            second + tendency(section_rim(second), speed_near, viscosity, heights)
        )
        per_column = jnp.repeat(shifts[step], heights)
        whole_blocks = per_column // block
        remainder = per_column - whole_blocks * block
        moved = third
        for level in range(levels):
            taken = whole_blocks >> level & 1 == 1
            arrived = shifted(moved, "azim", 1 << level)
            moved = jnp.where(taken[None, None, :], arrived, moved)
        preceding = shifted(moved, "azim", 1)
        joined = jnp.concatenate([preceding, moved], axis=1)
        state = slide_down(joined, remainder, block)[:, block:]
    return state


def winding(d):
    row, chip, core = d // 4, (d % 4) // 2, d % 2
    return row * 4 + ((row + chip) % 2) * 2 + core


def lateral_matrix(place, heights, n):
    total = n * OWNED
    half = OWNED // 2

    def places(axis):
        lane = lax.broadcasted_iota(jnp.int32, (3 * LANES, 2 * LANES), axis)
        height = lane % heights
        group = lane // heights
        tile, slot = group // OWNED, group % OWNED
        inner = jnp.where(slot < half, slot + OWNED, slot - OWNED)
        outer = jnp.where(slot < half, slot - OWNED, slot + OWNED)
        radius = jnp.where(tile == 0, slot, jnp.where(tile == 1, inner, outer))
        return height, radius + place * OWNED

    h_from, r_from = places(0)
    h_to, r_to = places(1)
    inside = (r_from >= 0) & (r_from < total) & (r_to >= 0) & (r_to < total)
    h_gap = jnp.abs(h_from - h_to)
    r_gap = jnp.abs(r_from - r_to)

    def one(condition):
        return jnp.where(condition, 1.0, 0.0)

    own = one(h_to == 0) + one(h_to == heights - 1) + one(r_to == 0) + one(r_to == total - 1) - 4.0
    weight = jnp.where(h_gap + r_gap == 0, own, one(h_gap + r_gap == 1))
    return jnp.where(inside, weight, 0.0).astype(jnp.bfloat16)


def disc_kernel(
    n,
    heights,
    cons,
    vel,
    visc_in,
    shifts_in,
    out,
    visc,
    shifts,
    s_own,
    u,
    mates,
    sides,
    packs,
    vp,
    vn,
    t1,
    t2,
    mat,
    obuf,
    a_send,
    a_recv,
    a_own,
    h_send,
    h_recv,
    x_send,
    x_recv,
    x_own,
    o_send,
    o_recv,
    o_own,
):
    fields, block, cols = cons.shape
    azim = n * block
    me = lax.axis_index("azim")
    place = winding(me)
    odd = lax.rem(place, 2)
    mate = winding(place + 1 - 2 * odd)
    beside = winding(lax.rem(place + n - 1 + 2 * odd, n))
    edge = (place == 0) | (place == n - 1)
    middle = n // 2
    central = (place == middle - 1) | (place == middle)

    barrier = pltpu.get_barrier_semaphore()

    def greet(k, carry):
        pl.semaphore_signal(barrier, inc=1, device_id={"azim": lax.rem(me + k, n)})
        return carry

    lax.fori_loop(1, n, greet, 0)
    pl.semaphore_wait(barrier, n - 1)

    def lanes(d):
        return pl.ds(pl.multiple_of(d * LANES, LANES), LANES)

    def rows(d):
        return pl.ds(pl.multiple_of(d * block, block), block)

    def share(plane, d):
        if isinstance(plane, int) and plane == fields:
            return vel.at[:, lanes(winding(d))]
        return cons.at[plane, :, lanes(winding(d))]

    def send_to(plane, to):
        pltpu.make_async_remote_copy(
            src_ref=share(plane, to),
            dst_ref=u.at[0, plane, rows(me), :],
            send_sem=a_send.at[plane],
            recv_sem=a_recv.at[plane],
            device_id={"azim": to},
        ).start()

    def cross_to(plane, side):
        taker = winding(middle - 1 + side)
        giver = winding(middle - side)
        there = pltpu.make_async_remote_copy(
            src_ref=share(plane, giver),
            dst_ref=sides.at[0, plane, rows(me), :],
            send_sem=x_send.at[plane],
            recv_sem=x_recv.at[plane],
            device_id={"azim": taker},
        )
        here = pltpu.make_async_copy(
            share(plane, giver), sides.at[0, plane, rows(me), :], x_own.at[plane]
        )
        return taker, there, here

    def send_in(plane):
        def one(k, carry):
            send_to(plane, lax.rem(me + k, n))
            return carry

        lax.fori_loop(1, n, one, 0)
        pltpu.make_async_copy(
            share(plane, me), u.at[0, plane, rows(me), :], a_own.at[plane]
        ).start()
        for side in (0, 1):
            taker, there, here = cross_to(plane, side)
            pl.when(taker != me)(there.start)
            pl.when(taker == me)(here.start)

    def send_at(f, carry):
        send_in(f)
        return carry

    row = me // 4
    inside = (row > 0) & (row < n // 4 - 1)
    early = jnp.where(inside, LOOK_INNER, fields)
    send_in(fields)
    lax.fori_loop(0, early, send_at, 0)

    scalars = (
        pltpu.make_async_copy(visc_in, visc, s_own.at[0]),
        pltpu.make_async_copy(shifts_in, shifts, s_own.at[1]),
    )
    for copy in scalars:
        copy.start()

    def all_in(plane):
        others = u.at[0, plane, pl.ds(0, azim - block), :]
        return pltpu.make_async_remote_copy(
            src_ref=others,
            dst_ref=others,
            send_sem=a_send.at[plane],
            recv_sem=a_recv.at[plane],
            device_id={"azim": mate},
        )

    def cross(plane, count):
        others = sides.at[0, plane, pl.ds(0, count * block), :]
        return pltpu.make_async_remote_copy(
            src_ref=others,
            dst_ref=others,
            send_sem=x_send.at[plane],
            recv_sem=x_recv.at[plane],
            device_id={"azim": mate},
        )

    held = azim // OWNED
    lane = lax.broadcasted_iota(jnp.int32, (azim, LANES), 1)
    lower = (lane < LANES // 2) == (odd == 0)
    spare = lane[:held] // heights == jnp.where(odd == 0, OWNED - 1, 0)

    def pack(step, plane):
        last = u[step, plane, azim - held :, :]
        for j in range(OWNED - 1):
            moved = pltpu.roll(last, LANES - (j + 1) * heights, 1)
            part = slice(j * held, (j + 1) * held)
            packs[step, plane, part, :] = jnp.where(spare, moved, u[step, plane, part, :])

    def unpack(step, plane):
        last = jnp.zeros((held, LANES), jnp.float32)
        for j in range(OWNED - 1):
            moved = pltpu.roll(sides[step, plane, j * held : (j + 1) * held, :], (j + 1) * heights, 1)
            here = lane[:held] // heights == j + 1 - odd
            last = jnp.where(here, moved, last)
        sides[step, plane, azim - held :, :] = last

    def across(step):
        return jnp.logical_not(edge | central) if step == 0 else jnp.logical_not(edge)

    def halo(step, plane):
        near = pltpu.make_async_remote_copy(
            src_ref=u.at[step, plane],
            dst_ref=mates.at[step, plane],
            send_sem=h_send.at[step, 0, plane],
            recv_sem=h_recv.at[step, 0, plane],
            device_id={"azim": mate},
        )
        far = pltpu.make_async_remote_copy(
            src_ref=packs.at[step, plane],
            dst_ref=sides.at[step, plane, pl.ds(0, azim - held), :],
            send_sem=h_send.at[step, 1, plane],
            recv_sem=h_recv.at[step, 1, plane],
            device_id={"azim": beside},
        )
        return near, far

    def halo_start(step, plane):
        near, far = halo(step, plane)
        near.start()

        @pl.when(across(step))
        def _():
            pack(step, plane)
            far.start()


    def halo_recv(step, plane):
        near, far = halo(step, plane)
        near.wait_recv()

        @pl.when(across(step))
        def _():
            far.wait_recv()
            unpack(step, plane)

        if step == 0:

            @pl.when(central)
            def _():
                own = sides.at[0, plane, rows(me), :]
                pltpu.make_async_copy(own, own, x_own.at[plane]).wait()
                cross(plane, n - 1).wait_recv()

    def halo_sent(step, plane):
        near, far = halo(step, plane)
        near.wait_send()
        pl.when(across(step))(far.wait_send)

    def arrive(plane):
        pltpu.make_async_copy(
            u.at[0, plane, rows(me), :], u.at[0, plane, rows(me), :], a_own.at[plane]
        ).wait()
        all_in(plane).wait_recv()
        halo_start(0, plane)
        later = early if isinstance(plane, int) and plane == fields else plane + early + 1
        pl.when(later < fields)(lambda: send_in(later))

    def send_out(f):
        def one(to, carry):
            @pl.when(to != me)
            def _():
                pltpu.make_async_remote_copy(
                    src_ref=obuf.at[f, rows(to), :],
                    dst_ref=out.at[f, :, lanes(place)],
                    send_sem=o_send.at[f],
                    recv_sem=o_recv.at[f],
                    device_id={"azim": to},
                ).start()

            return carry

        lax.fori_loop(0, n, one, 0)

    def own_out(f):
        return pltpu.make_async_copy(
            obuf.at[f, rows(me), :], out.at[f, :, lanes(place)], o_own.at[f]
        )

    def each(body, count=fields):
        def one(f, carry):
            body(f)
            return carry

        lax.fori_loop(0, count, one, 0)

    def clear(tile):
        def one(plane, carry):
            for step in range(STEPS):
                tile[step, plane] = jnp.zeros((azim, LANES), jnp.float32)
            return carry

        lax.fori_loop(0, fields + 1, one, 0)

    pl.when(edge)(lambda: clear(sides))
    mat[...] = lateral_matrix(place, heights, n)

    def tiles(step, plane):
        own, close, side = u[step, plane], mates[step, plane], sides[step, plane]
        near = jnp.concatenate([own, jnp.where(lower, close, side)], axis=1)
        return near, jnp.where(lower, side, close)

    def ahead_one(x):
        return pltpu.roll(x, azim - 1, 0)

    def back_one(x):
        return pltpu.roll(x, 1, 0)

    def halves(x):
        high = x.astype(jnp.bfloat16)
        return high, (x - high.astype(jnp.float32)).astype(jnp.bfloat16)

    def lateral(x, count):
        parts = []
        size = azim // 2
        for k in range(2):
            both = jnp.concatenate(halves(x[k * size : (k + 1) * size]), axis=0)
            y = jnp.dot(both, mat[: 2 * LANES, :count], preferred_element_type=jnp.float32)
            parts.append(y[:size] + y[size:])
        return jnp.concatenate(parts, axis=0)

    def change(x, spread, nu):
        count = spread.shape[1]
        x = x[:, :count]
        d = x - back_one(x)
        dp = ahead_one(d)
        low = jnp.minimum(d, dp)
        high = jnp.maximum(d, dp)
        half = 0.5 * (jnp.maximum(low, 0.0) + jnp.minimum(high, 0.0))
        p = vp[:, :count] * (x + half)
        q = vn[:, :count] * (x - half)
        flow = (p - q) + (ahead_one(q) - back_one(p))
        return x + (nu * ((dp - d) + spread) - flow)

    def advance(step, f):
        nu = visc[f]
        near, far = tiles(step, f)
        rim = mat[2 * LANES :, :]
        spread = lateral(near, 2 * LANES) + jnp.dot(
            jnp.concatenate(halves(far), axis=1),
            jnp.concatenate([rim, rim], axis=0),
            preferred_element_type=jnp.float32,
        )
        t1[...] = change(near, spread, nu)
        x = t1[...]
        t2[...] = 0.75 * near + 0.25 * change(x, lateral(x, 2 * LANES), nu)
        x = t2[...]
        y = (1.0 / 3.0) * near[:, :LANES] + (2.0 / 3.0) * change(x, lateral(x, LANES), nu)
        slot = lax.broadcasted_iota(jnp.int32, (SUBLANES, LANES), 1) // heights
        amount = jnp.zeros((SUBLANES, LANES), jnp.int32)
        for r in range(OWNED):
            amount = jnp.where(slot == r, shifts[step, place * OWNED + r], amount)
        for bit in range(azim.bit_length() - 1):
            taken = ((amount >> bit) & 1 == 1)[:1]
            taken = jnp.broadcast_to(taken, (azim, LANES))
            y = jnp.where(taken, pltpu.roll(y, 1 << bit, 0), y)
        if step + 1 < STEPS:
            u[step + 1, f] = y
        else:
            obuf[f] = y

    arrive(fields)
    for f in range(AHEAD):
        arrive(f)
    for copy in scalars:
        copy.wait()
    def faces():
        halo_recv(0, fields)
        v, _ = tiles(0, fields)
        speed = 0.5 * (v + back_one(v))
        vn[...] = jnp.minimum(speed, 0.0)
        vp[...] = ahead_one(jnp.maximum(speed, 0.0))

    def work(i):
        @pl.when(i + AHEAD < fields)
        def _():
            arrive(i + AHEAD)

        pl.when(i == 0)(faces)

        @pl.when(i < fields)
        def _():
            halo_recv(0, i)
            advance(0, i)
            halo_start(1, i)

        @pl.when(i >= LAG)
        def _():
            halo_recv(1, i - LAG)
            advance(1, i - LAG)
            own_out(i - LAG).start()
            send_out(i - LAG)

    each(work, fields + LAG)

    def sent(plane):
        all_in(plane).wait_send()
        pl.when(central)(cross(plane, 1).wait_send)
        pl.when(jnp.logical_not(central))(cross(plane, 2).wait_send)
        halo_sent(0, plane)

    each(sent, fields + 1)

    def finish(f):
        halo_sent(1, f)
        own_out(f).wait()
        others = obuf.at[f, pl.ds(0, azim - block), :]
        done = pltpu.make_async_remote_copy(
            src_ref=others,
            dst_ref=others,
            send_sem=o_send.at[f],
            recv_sem=o_recv.at[f],
            device_id={"azim": mate},
        )
        done.wait_send()
        done.wait_recv()

    each(finish)


def by_radius(conserved, velocity, viscosity, shifts):
    fields, block, cols = conserved.shape
    n = lax.axis_size("azim")
    heights = cols // shifts.shape[1]
    azim = n * block
    f32 = jnp.float32
    dma = pltpu.SemaphoreType.DMA
    operands = (conserved, velocity, viscosity, shifts)
    held = [pltpu.with_memory_space_constraint(x, pltpu.HBM) for x in operands]
    return pl.pallas_call(
        functools.partial(disc_kernel, n, heights),
        out_shape=pltpu.VMEM(conserved.shape, f32),
        in_specs=[pl.BlockSpec(memory_space=pltpu.HBM)] * 4,
        out_specs=pl.BlockSpec(memory_space=pltpu.VMEM),
        scratch_shapes=[
            pltpu.SMEM(viscosity.shape, f32),
            pltpu.SMEM(shifts.shape, jnp.int32),
            dma((2,)),
            pltpu.VMEM((STEPS, fields + 1, azim, LANES), f32),
            pltpu.VMEM((STEPS, fields + 1, azim, LANES), f32),
            pltpu.VMEM((STEPS, fields + 1, azim, LANES), f32),
            pltpu.VMEM((STEPS, fields + 1, azim - azim // OWNED, LANES), f32),
            pltpu.VMEM((azim, 2 * LANES), f32),
            pltpu.VMEM((azim, 2 * LANES), f32),
            pltpu.VMEM((azim, 2 * LANES), f32),
            pltpu.VMEM((azim, 2 * LANES), f32),
            pltpu.VMEM((3 * LANES, 2 * LANES), jnp.bfloat16),
            pltpu.VMEM((fields, azim, LANES), f32),
            dma((fields + 1,)),
            dma((fields + 1,)),
            dma((fields + 1,)),
            dma((STEPS, 2, fields + 1)),
            dma((STEPS, 2, fields + 1)),
            dma((fields + 1,)),
            dma((fields + 1,)),
            dma((fields + 1,)),
            dma((fields,)),
            dma((fields,)),
            dma((fields,)),
        ],
        compiler_params=pltpu.CompilerParams(
            collective_id=0, has_side_effects=True, vmem_limit_bytes=16 * 1024 * 1024
        ),
    )(*held)


def local(conserved, velocity, viscosity, shifts):
    fields, block, cols = conserved.shape
    n = lax.axis_size("azim")
    heights = cols // shifts.shape[1]
    fits = (
        n == 16
        and n * block == LANES
        and block == SUBLANES
        and cols == n * LANES
        and heights * OWNED == LANES
    )
    if fits:
        return by_radius(conserved, velocity, viscosity, shifts)
    return by_azimuth(conserved, velocity, viscosity, shifts)


def solution(mesh):
    in_specs = (
        P(None, ("groups", "azim"), None),
        P(("groups", "azim"), None),
        P(),
        P("groups", None),
    )
    out_specs = P(None, ("groups", "azim"), None)
    return jax.shard_map(local, mesh=mesh, in_specs=in_specs, out_specs=out_specs, check_vma=False)
```
